256 devices in a mesh: row: 32 (over z_lo, x, core), rhs: 8 (over y, z_hi).
Axes of the slice: x: 4, y: 4, z: 8 (z_hi: 2, z_lo: 4; z = z_hi * 4 + z_lo), core: 2. Of those that a mesh axis runs over, the one named last changes fastest.
Arguments:
- rhs_in: float32 [2, 1024, 16384], P(None, ('rhs', 'row')), may hold values from -6 to 6
- pivots: int32 [16384], replicated, may hold values from 0 to 16383, each once
- owners: int32 [32], replicated, may hold values from 0 to 31, each once
- panel_first: float32 [2, 16384, 512], P(None, 'row'), may hold values from -0.1875 to 0.1875
- panel_second: float32 [2, 16384, 512], P(None, 'row'), may hold values from -0.1875 to 0.1875
- inverse_first: float32 [2, 512, 512], replicated, may hold values from -0.1875 to 0.1875
- inverse_second: float32 [2, 512, 512], replicated, may hold values from -0.1875 to 0.1875
Outputs:
- solved_rhs: float32 [2, 1024, 16384], P(None, 'rhs', 'row')
The draws below stay inside these ranges and needn't reach their ends.
Inputs may be any that keep to these rules, and one draw needn't show every extreme that they name: `pivots`: each row number occurs once. `owners`: each device index along row occurs once.
All inputs are finite; a program needn't handle non-finite values.
Results may differ from the reference program's by a relative error of at most 0.0001.
Values sent between devices are 32-bit elements; how exact they have to be, the bound alone decides.
No kernel may reach another device: no remote copies, remote signals or barrier semaphores. Data moves between devices by JAX's collectives and lax.ppermute only.
A program may use at most 128 MiB of HBM per device.

```python
import jax
import jax.numpy as jnp
from jax import lax

BLK = 512
NRHS = 1024
ROWS = 16384
N_ROW = 32


def block_levels(stream_key, extent, split, low, high):
    gain = 1.0
    for position, shards_of in split:
        steps = jax.random.uniform(jax.random.fold_in(jax.random.fold_in(stream_key, 6), position), (shards_of,), jnp.float32, low / len(split), high / len(split))
        gain = gain * jnp.repeat(jnp.exp(steps), extent[position] // shards_of).reshape((-1,) + (1,) * (len(extent) - 1 - position))
    return gain


def normal_values(stream_key, dims, width, most, pieces=(), held_as=jnp.bfloat16):
    result = jax.random.normal(stream_key, dims, jnp.float32) * width
    if len(pieces) > 0:
        result = block_levels(stream_key, dims, pieces, -0.22, 0.18) * result
    return jnp.clip(result, min=-most, max=most).astype(held_as)


def setup_inputs(seed: int = 0) -> dict:
    arg_keys = jax.random.split(jax.random.key(seed), 8)
    return {
        "rhs_in": normal_values(arg_keys[0], (2, NRHS, ROWS), 1.0, 6.0, ((1, 256),), jnp.float32),
        "pivots": jax.random.permutation(arg_keys[1], ROWS).astype(jnp.int32),
        "owners": jax.random.permutation(arg_keys[2], N_ROW).astype(jnp.int32),
        "panel_first": normal_values(arg_keys[3], (2, ROWS, BLK), (2 * BLK) ** -0.5, 0.1875, ((1, 32),), jnp.float32),
        "panel_second": normal_values(arg_keys[4], (2, ROWS, BLK), (2 * BLK) ** -0.5, 0.1875, ((1, 32),), jnp.float32),
        "inverse_first": normal_values(arg_keys[5], (2, BLK, BLK), (2 * BLK) ** -0.5, 0.1875, (), jnp.float32),
        "inverse_second": normal_values(arg_keys[6], (2, BLK, BLK), (2 * BLK) ** -0.5, 0.1875, (), jnp.float32),
    }


def complex_product(operand, matrix):
    contract = (((1,), (1,)), ((), ()))

    def multiply(first, second):
        return lax.dot_general(first, second, contract, precision=lax.Precision.HIGHEST, preferred_element_type=jnp.float32)

    real_part = multiply(operand[0], matrix[0]) - multiply(operand[1], matrix[1])
    imag_part = multiply(operand[0], matrix[1]) + multiply(operand[1], matrix[0])
    return jnp.stack([real_part, imag_part])


def reference(rhs_in, pivots, owners, panel_first, panel_second, inverse_first, inverse_second):
    blocks = owners.shape[0]
    slot_block = jnp.zeros((blocks,), jnp.int32).at[owners].set(jnp.arange(blocks, dtype=jnp.int32))
    row_index = (slot_block[:, None] * BLK + jnp.arange(BLK, dtype=jnp.int32)[None, :]).reshape(-1)
    current = jnp.take(rhs_in, jnp.take(pivots, row_index), axis=2)
    row_block = jnp.repeat(slot_block, BLK)
    sections = ((panel_first, inverse_first), (panel_second, inverse_second))
    for block_step in range(2):
        panel_rows, inverse = sections[block_step]
        holder = (owners[block_step] * BLK).astype(jnp.int32)
        rhs_block = lax.dynamic_slice_in_dim(current, holder, BLK, 2)
        solution = complex_product(rhs_block, inverse)
        update = complex_product(solution, panel_rows)
        later = (row_block > block_step)[None, None, :]
        current = jnp.where(later, current - update, current)
        current = lax.dynamic_update_slice_in_dim(current, solution, holder, 2)
    return current
```

```python
import functools

import jax
import jax.numpy as jnp
from jax import lax
from jax.experimental import pallas as pl
from jax.experimental.pallas import tpu as pltpu
from jax.sharding import Mesh, PartitionSpec as P

F32 = jnp.float32
BF16 = jnp.bfloat16
NT = (((1,), (1,)), ((), ()))
NN = (((1,), (0,)), ((), ()))


def split(v):
    high = v.astype(BF16)
    return high, (v - high.astype(F32)).astype(BF16)


def turned(v):
    tiles = v.reshape(v.shape[0] // 8, 8, v.shape[1])
    row = lax.broadcasted_iota(jnp.int32, tiles.shape, 1)
    swapped = pltpu.roll(tiles, 4, 1)
    return jnp.where(row < 4, -swapped, swapped).reshape(v.shape)


def dot(a, b, dims=NT):
    return lax.dot_general(a, b, dims, preferred_element_type=F32)


def gather_columns(left, pivots):
    n = pivots.shape[1]
    major = pivots >> 7
    minor = pivots & 127
    pick = (lax.broadcasted_iota(jnp.int32, (128, n), 0) == major).astype(F32).astype(BF16)
    product = dot(left, jnp.concatenate([pick, pick], 0), NN).reshape(8, 16, 8, n)
    row = lax.broadcasted_iota(jnp.int32, (8, n), 0)
    found = jnp.zeros((8, 8, n), F32)
    for j in range(16):
        found = jnp.where((row + 8 * j == minor)[None], product[:, j], found)
    return found.sum(axis=1)


def pieces_kernel(place_ref, panel_ref, out_ref):
    half = place_ref[1]
    for z in range(4):
        for k in range(8):
            start = pl.multiple_of(64 * k + 16 * z + 8 * half, 8)
            for part in range(2):
                out_ref[z * 8 + k, part] = panel_ref[part, pl.ds(start, 8), :]


def make_pieces(place, panel):
    return pl.pallas_call(
        pieces_kernel,
        grid_spec=pltpu.PrefetchScalarGridSpec(
            num_scalar_prefetch=1,
            grid=(1,),
            in_specs=[pl.BlockSpec((2, 512, 128), lambda i, place: (0, 0, place[0]))],
            out_specs=pl.BlockSpec((32, 2, 8, 128), lambda i, place: (0, 0, 0, 0)),
        ),
        out_shape=jax.ShapeDtypeStruct((32, 2, 8, 128), F32),
        name="pieces",
    )(place, panel)


def head_kernel(rhs_ref, pivots_ref, inverse_ref, left_ref, out_ref):
    for part in range(2):
        for c in range(4):
            r = part * 4 + c
            high, low = split(rhs_ref[part, :, c, :].T)
            left_ref[pl.ds(128 * r, 128), 0:128] = high
            left_ref[pl.ds(128 * r, 128), 128:256] = low
    left = left_ref[...]
    first = [gather_columns(left, pivots_ref[0:1, 256 * k : 256 * k + 256]) for k in range(2)]
    second = [gather_columns(left, pivots_ref[1:2, 256 * k : 256 * k + 256]) for k in range(2)]
    first = jnp.concatenate(first, 1)
    operand = jnp.concatenate([first, turned(first)], 1)
    high, low = split(operand)
    w_high, w_low = split(jnp.concatenate([inverse_ref[0], inverse_ref[1]], 1))
    both = dot(jnp.concatenate([high, low], 0), w_high)
    solved = both[0:8] + both[8:16] + dot(high, w_low)
    second = jnp.concatenate(second, 1)
    for k in range(4):
        out_ref[k, 0] = solved
        out_ref[k, 1] = second


def head(rhs, pivots, inverse):
    return pl.pallas_call(
        head_kernel,
        grid=(1,),
        in_specs=[
            pl.BlockSpec((2, 128, 4, 128), lambda i: (0, 0, 0, 0)),
            pl.BlockSpec((8, 512), lambda i: (0, 0)),
            pl.BlockSpec((2, 512, 512), lambda i: (0, 0, 0)),
        ],
        out_specs=[
            pl.BlockSpec((1024, 256), lambda i: (0, 0)),
            pl.BlockSpec((4, 2, 8, 512), lambda i: (0, 0, 0, 0)),
        ],
        out_shape=[
            jax.ShapeDtypeStruct((1024, 256), BF16),
            jax.ShapeDtypeStruct((4, 2, 8, 512), F32),
        ],
        name="head",
    )(rhs, pivots, inverse)


def gather_kernel(owners_ref, left_ref, pivots_ref, *rest):
    out_ref = rest[-1]
    left = left_ref[...]
    for k in range(2):
        out_ref[0, :, 256 * k : 256 * k + 256] = gather_columns(left, pivots_ref[0, :, 256 * k : 256 * k + 256])


def gather(owners, left, pivots, start, count, into=None):
    specs = [
        pl.BlockSpec((1024, 256), lambda i, owners: (0, 0)),
        pl.BlockSpec((1, 1, 512), lambda i, owners: (i + start, 0, 0)),
    ]
    operands = [owners, left, pivots]
    aliases = {}
    if into is not None:
        specs.append(pl.BlockSpec(memory_space=pl.ANY))
        operands.append(into)
        aliases = {3: 0}
    return pl.pallas_call(
        gather_kernel,
        grid_spec=pltpu.PrefetchScalarGridSpec(
            num_scalar_prefetch=1,
            grid=(count,),
            in_specs=specs,
            out_specs=pl.BlockSpec((1, 8, 512), lambda i, owners: (owners[i + start], 0, 0)),
        ),
        out_shape=jax.ShapeDtypeStruct((32, 8, 512), F32),
        input_output_aliases=aliases,
        name="gather_blocks",
    )(*operands)


def operands_kernel(all_ref, high_ref, low_ref):
    for k in range(0, 32, 2):
        a, b = k // 16, (k // 4) % 4
        z = k % 4
        v = jnp.concatenate([all_ref[a, b, z, 0], all_ref[a, b, z + 1, 0]], 0)
        high, low = split(jnp.concatenate([v, turned(v)], 1))
        high_ref[pl.ds(8 * k, 16), :] = high
        low_ref[pl.ds(8 * k, 16), :] = low


def make_operands(gathered):
    return pl.pallas_call(
        operands_kernel,
        grid=(1,),
        in_specs=[pl.BlockSpec((2, 4, 4, 1, 8, 512), lambda i: (0, 0, 0, 0, 0, 0))],
        out_specs=[pl.BlockSpec((256, 1024), lambda i: (0, 0))] * 2,
        out_shape=[jax.ShapeDtypeStruct((256, 1024), BF16)] * 2,
        name="operands",
    )(gathered)


def cross_kernel(pieces_ref, high_ref, low_ref, out_ref, panel_ref):
    for z in range(4):
        for r in range(8):
            o, cb = 2 * z + r // 4, r % 4
            for part in range(2):
                panel_ref[pl.ds(8 * o, 8), pl.ds(512 * part + 128 * cb, 128)] = pieces_ref[z * 8 + r, part]
    q_high, q_low = split(panel_ref[...])
    both = dot(jnp.concatenate([q_high, q_low], 0), high_ref[...])
    value = both[0:64] + both[64:128] + dot(q_high, low_ref[...])
    for k in range(8):
        out_ref[k] = value


def cross(pieces, high, low):
    return pl.pallas_call(
        cross_kernel,
        out_shape=jax.ShapeDtypeStruct((8, 64, 256), F32),
        scratch_shapes=[pltpu.VMEM((64, 1024), F32)],
        name="cross",
    )(pieces, high, low)


def weights(ref):
    return split(jnp.concatenate([ref[0], ref[1]], 1))


def triple(high, low, w_high, w_low):
    return dot(high, w_high) + (dot(low, w_high) + dot(high, w_low))


def base_kernel(block_ref, current_ref, gathered_ref, high_ref, low_ref, panel_ref, out_ref):
    block = block_ref[0]
    w_high, w_low = weights(panel_ref)
    update = triple(high_ref[...], low_ref[...], w_high, w_low)
    for k in range(32):
        a, b, z = k // 16, (k // 4) % 4, k % 4
        d = z * 8 + b * 2 + a
        later = current_ref[d] - update[8 * k : 8 * k + 8]
        out_ref[pl.ds(8 * k, 8), :] = jnp.where(block == 0, gathered_ref[a, b, z, 0], later)


def make_base(block, current, gathered, high, low, panel):
    vmem = pl.BlockSpec(memory_space=pltpu.VMEM)
    return pl.pallas_call(
        base_kernel,
        in_specs=[pl.BlockSpec(memory_space=pltpu.SMEM)] + [vmem] * 5,
        out_shape=jax.ShapeDtypeStruct((256, 512), F32),
        name="base",
    )(block, current, gathered, high, low, panel)


def tail_kernel(block_ref, base_ref, gathered_ref, cross_ref, inverse_ref, panel_ref, out_ref):
    block = block_ref[0]
    other = jnp.concatenate([gathered_ref[k // 16, (k // 4) % 4, k % 4, 1] for k in range(32)], 0)
    value = other - cross_ref[...].reshape(512, 256).T
    high, low = split(jnp.concatenate([value, turned(value)], 1))
    solved = triple(high, low, *weights(inverse_ref))
    high, low = split(jnp.concatenate([solved, turned(solved)], 1))
    update = triple(high, low, *weights(panel_ref))
    base = base_ref[...]
    result = jnp.where(block > 1, base - update, jnp.where(block == 1, solved, base))
    for k in range(32):
        a, b, z = k // 16, (k // 4) % 4, k % 4
        d = z * 8 + b * 2 + a
        out_ref[0, pl.ds(4 * d, 4), :] = result[8 * k : 8 * k + 4]
        out_ref[1, pl.ds(4 * d, 4), :] = result[8 * k + 4 : 8 * k + 8]


def tail(block, base, gathered, crossed, inverse, panel):
    vmem = pl.BlockSpec(memory_space=pltpu.VMEM)
    return pl.pallas_call(
        tail_kernel,
        in_specs=[pl.BlockSpec(memory_space=pltpu.SMEM)] + [vmem] * 5,
        out_shape=jax.ShapeDtypeStruct((2, 128, 512), F32),
        name="tail",
    )(block, base, gathered, crossed, inverse, panel)


def exchange(v, axis):
    return lax.all_to_all(v, axis, 0, 0, tiled=True)


def repeat(v, n):
    return jnp.broadcast_to(v[None], (n,) + v.shape)


def shards(rhs_in, pivots, owners, panel_first, panel_second, inverse_first, inverse_second):
    row = ("z", "x", "c")
    me = lax.axis_index(row)
    replica = lax.axis_index("rhs")
    block = jnp.sum(jnp.where(owners == me, jnp.arange(32, dtype=jnp.int32), 0)).reshape(1)
    place = jnp.stack([replica & 3, replica >> 2]).astype(jnp.int32)
    rhs = rhs_in.reshape(2, 4, 128, 128).transpose(0, 2, 1, 3)
    piv = pivots.reshape(32, 512)

    pieces = exchange(make_pieces(place, panel_first), row)
    left, mine = head(rhs, piv, inverse_first)
    gathered = exchange(mine, "z")
    piece = lax.dynamic_index_in_dim(pieces, owners[1], 0, keepdims=False)
    pieces = exchange(repeat(piece, 32), ("z", "rhs"))
    gathered = exchange(repeat(gathered, 4), "x")
    blocks = gather(owners, left, piv.reshape(32, 1, 512), 2, 15)
    gathered = exchange(repeat(gathered, 2), "c")
    blocks = gather(owners, left, piv.reshape(32, 1, 512), 17, 15, blocks)
    current = exchange(blocks, row)
    high, low = make_operands(gathered)
    crossed = exchange(cross(pieces, high, low), ("x", "c"))
    base = make_base(block, current, gathered, high, low, panel_first)
    return tail(block, base, gathered, crossed, inverse_second, panel_second)


def solution(mesh):
    fine = Mesh(mesh.devices.reshape(4, 4, 2, 8), ("z", "x", "c", "rhs"))
    row = ("z", "x", "c")
    return jax.shard_map(
        shards,
        mesh=fine,
        in_specs=(
            P(None, ("rhs",) + row, None),
            P(),
            P(),
            P(None, row, None),
            P(None, row, None),
            P(),
            P(),
        ),
        out_specs=P(None, "rhs", row),
        check_vma=False,
    )
```

```python
import functools

import jax
import jax.numpy as jnp
from jax import lax
from jax.experimental import pallas as pl
from jax.experimental.pallas import tpu as pltpu
from jax.sharding import Mesh, PartitionSpec as P


F32 = jnp.float32
BF16 = jnp.bfloat16
NT = (((1,), (1,)), ((), ()))
NN = (((1,), (0,)), ((), ()))


def split(v):
    high = v.astype(BF16)
    return high, (v - high.astype(F32)).astype(BF16)


def turned(v):
    tiles = v.reshape(v.shape[0] // 8, 8, v.shape[1])
    row = lax.broadcasted_iota(jnp.int32, tiles.shape, 1)
    swapped = pltpu.roll(tiles, 4, 1)
    return jnp.where(row < 4, -swapped, swapped).reshape(v.shape)


def dot(a, b, dims=NT):
    return lax.dot_general(a, b, dims, preferred_element_type=F32)


def gather_columns(left, pivots):
    n = pivots.shape[1]
    major = pivots >> 7
    minor = pivots & 127
    pick = (lax.broadcasted_iota(jnp.int32, (128, n), 0) == major).astype(F32).astype(BF16)
    product = dot(left, jnp.concatenate([pick, pick], 0), NN).reshape(8, 16, 8, n)
    row = lax.broadcasted_iota(jnp.int32, (8, n), 0)
    found = jnp.zeros((8, 8, n), F32)
    for j in range(16):
        found = jnp.where((row + 8 * j == minor)[None], product[:, j], found)
    return found.sum(axis=1)


VMEM = pl.BlockSpec(memory_space=pltpu.VMEM)
SMEM = pl.BlockSpec(memory_space=pltpu.SMEM)
HBM = pl.BlockSpec(memory_space=pltpu.HBM)
SMALL = pltpu.CompilerParams(vmem_limit_bytes=24 << 20)


def held(v):
    return pltpu.with_memory_space_constraint(v, pltpu.VMEM)


def head_kernel(
    place_ref, panel_ref, rhs_hbm, pivots_ref, inverse_hbm, left_ref, pieces_ref, own_ref, rhs_ref, inverse_ref, sem
):
    fetch_rhs = pltpu.make_async_copy(rhs_hbm, rhs_ref, sem.at[32])
    fetch_inverse = pltpu.make_async_copy(inverse_hbm, inverse_ref, sem.at[33])
    fetch_rhs.start()
    column = pl.multiple_of(128 * place_ref[0], 128)
    copies = []
    for z in range(4):
        for k in range(8):
            source = panel_ref.at[:, pl.ds(8 * k + 2 * z, 2), :, pl.ds(column, 128)]
            copies.append(pltpu.make_async_copy(source, pieces_ref.at[z * 8 + k], sem.at[z * 8 + k]))
    for copy in copies:
        copy.start()
    fetch_inverse.start()
    fetch_rhs.wait()
    for part in range(2):
        for c in range(4):
            r = part * 4 + c
            high, low = split(rhs_ref[part, :, c, :].T)
            left_ref[pl.ds(128 * r, 128), 0:128] = high
            left_ref[pl.ds(128 * r, 128), 128:256] = low
    left = left_ref[...]
    first = jnp.concatenate([gather_columns(left, pivots_ref[0, :, 256 * k : 256 * k + 256]) for k in range(2)], 1)
    second = jnp.concatenate([gather_columns(left, pivots_ref[1, :, 256 * k : 256 * k + 256]) for k in range(2)], 1)
    own_ref[1] = second
    high, low = split(jnp.concatenate([first, turned(first)], 1))
    fetch_inverse.wait()
    w_high, w_low = split(jnp.concatenate([inverse_ref[0], inverse_ref[1]], 1))
    both = dot(jnp.concatenate([high, low], 0), w_high)
    own_ref[0] = both[0:8] + both[8:16] + dot(high, w_low)
    for copy in copies:
        copy.wait()


def in_hbm(v):
    return pltpu.with_memory_space_constraint(v, pltpu.HBM)


def head(place, panel, rhs, pivots, inverse):
    return pl.pallas_call(
        head_kernel,
        in_specs=[SMEM, HBM, HBM, VMEM, HBM],
        out_specs=[VMEM, VMEM, VMEM],
        out_shape=[
            pltpu.VMEM((1024, 256), BF16),
            jax.ShapeDtypeStruct((32, 2, 2, 8, 128), F32),
            pltpu.VMEM((2, 8, 512), F32),
        ],
        scratch_shapes=[
            pltpu.VMEM((2, 128, 4, 128), F32),
            pltpu.VMEM((2, 512, 512), F32),
            pltpu.SemaphoreType.DMA((34,)),
        ],
        name="head",
        compiler_params=SMALL,
    )(place, in_hbm(panel), in_hbm(rhs), pivots, in_hbm(inverse))


def gather_kernel(start, count, owners_ref, left_ref, pivots_ref, *rest):
    out_ref, stage_ref, sem = rest[-3:]

    def send(i):
        return pltpu.make_async_copy(stage_ref.at[i], out_ref.at[owners_ref[start + i]], sem.at[i])

    def step(i, carry):
        left = left_ref[...]
        for k in range(2):
            at = slice(256 * k, 256 * k + 256)
            stage_ref[i, :, at] = gather_columns(left, pivots_ref[start + i, :, at])
        send(i).start()
        return carry

    lax.fori_loop(0, count, step, 0, unroll=3)
    for i in range(count):
        send(i).wait()


def gather(owners, left, pivots, start, count, into=None):
    operands = [owners, held(left), pivots]
    specs = [SMEM, VMEM, VMEM]
    aliases = {}
    if into is not None:
        operands.append(into)
        specs.append(HBM)
        aliases = {3: 0}
    return pl.pallas_call(
        functools.partial(gather_kernel, start, count),
        in_specs=specs,
        out_specs=HBM,
        out_shape=pltpu.HBM((32, 8, 512), F32),
        scratch_shapes=[pltpu.VMEM((count, 8, 512), F32), pltpu.SemaphoreType.DMA((count,))],
        input_output_aliases=aliases,
        name="gather_blocks",
        compiler_params=SMALL,
    )(*operands)


def pick_kernel(owners_ref, all_ref, out_ref):
    out_ref[...] = all_ref[owners_ref[1]]


def pick(owners, everything):
    return pl.pallas_call(
        pick_kernel,
        in_specs=[SMEM, VMEM],
        out_specs=VMEM,
        out_shape=pltpu.VMEM((2, 2, 8, 128), F32),
        name="pick",
        compiler_params=SMALL,
    )(owners, held(everything))


def triple(high, low, ref):
    n = high.shape[0]
    w_high, w_low = split(jnp.concatenate([ref[0], ref[1]], 1))
    both = dot(jnp.concatenate([high, low], 0), w_high)
    return both[:n] + (both[n:] + dot(high, w_low))


def operands_kernel(me_ref, mine_ref, other_ref, high_ref, low_ref, solved_ref, second_ref):
    me = me_ref[0]
    even = (me & 1) == 0
    for j in range(16):
        at = pl.ds(16 * j, 16)
        k = (me >> 1) ^ j
        mine, other = mine_ref[k & 3, k >> 2], other_ref[k & 3, k >> 2]
        first, last = jnp.where(even, mine, other), jnp.where(even, other, mine)
        v = jnp.concatenate([first[0], last[0]], 0)
        high, low = split(jnp.concatenate([v, turned(v)], 1))
        high_ref[at, :] = high
        low_ref[at, :] = low
        solved_ref[at, :] = v
        second_ref[at, :] = jnp.concatenate([first[1], last[1]], 0)


def make_operands(me, mine, other):
    return pl.pallas_call(
        operands_kernel,
        in_specs=[SMEM, VMEM, VMEM],
        out_specs=[VMEM] * 4,
        out_shape=[pltpu.VMEM((256, 1024), BF16)] * 2 + [pltpu.VMEM((256, 512), F32)] * 2,
        name="operands",
        compiler_params=SMALL,
    )(me, held(mine), held(other))


def update_kernel(me_ref, owners_ref, high_ref, low_ref, solved_ref, panel_hbm, out_ref, panel_ref, sem):
    fetch = pltpu.make_async_copy(panel_hbm, panel_ref, sem)
    fetch.start()
    fetch.wait()
    update = triple(high_ref[...], low_ref[...], panel_ref)
    out_ref[...] = jnp.where(owners_ref[0] == me_ref[0], -solved_ref[...], update)


def make_update(me, owners, high, low, solved, panel):
    return pl.pallas_call(
        update_kernel,
        in_specs=[SMEM, SMEM, VMEM, VMEM, VMEM, HBM],
        out_specs=VMEM,
        out_shape=pltpu.VMEM((256, 512), F32),
        scratch_shapes=[pltpu.VMEM((2, 512, 512), F32), pltpu.SemaphoreType.DMA],
        name="update",
        compiler_params=SMALL,
    )(me, owners, held(high), held(low), held(solved), in_hbm(panel))


def cross_kernel(me_ref, place_ref, pieces_ref, high_ref, low_ref, out_ref, panel_ref):
    for z in range(4):
        for y in range(4):
            for part in range(2):
                for o in range(2):
                    at = pl.ds(512 * part + 128 * y, 128)
                    piece = pieces_ref[place_ref[0] ^ y, (me_ref[0] >> 3) ^ z, part, o]
                    panel_ref[pl.ds(16 * z + 8 * o, 8), at] = piece
    q_high, q_low = split(panel_ref[...])
    both = dot(jnp.concatenate([q_high, q_low], 0), high_ref[...])
    out_ref[...] = both[0:64] + both[64:128] + dot(q_high, low_ref[...])


def cross(me, place, pieces, high, low):
    return pl.pallas_call(
        cross_kernel,
        in_specs=[SMEM, SMEM] + [VMEM] * 3,
        out_specs=VMEM,
        out_shape=pltpu.VMEM((64, 256), F32),
        scratch_shapes=[pltpu.VMEM((64, 1024), F32)],
        name="cross",
        compiler_params=SMALL,
    )(me, place, held(pieces), held(high), held(low))


def tail_kernel(
    me_ref, owners_ref, base_ref, second_ref, mine_ref, other_ref, inverse_ref, panel_hbm, out_ref,
    cross_ref, panel_ref, sem,
):
    fetch = pltpu.make_async_copy(panel_hbm, panel_ref, sem)
    fetch.start()
    me = me_ref[0]
    core = me & 1
    for x in range(4):
        k = ((me >> 1) & 3) ^ x
        cross_ref[pl.ds(pl.multiple_of(128 * x + 64 * core, 64), 64), :] = mine_ref[k]
        cross_ref[pl.ds(pl.multiple_of(128 * x + 64 - 64 * core, 64), 64), :] = other_ref[k]

    def product(value, ref):
        return triple(*split(jnp.concatenate([value, turned(value)], 1)), ref)

    solved = product(second_ref[...] - cross_ref[...].T, inverse_ref)
    fetch.wait()
    update = base_ref[...] + jnp.where(owners_ref[0] == me, 0.0, product(solved, panel_ref))
    out_ref[...] = jnp.where(owners_ref[1] == me, -solved, update)


def tail(me, owners, base, second, mine, other, inverse, panel):
    return pl.pallas_call(
        tail_kernel,
        in_specs=[SMEM, SMEM] + [VMEM] * 5 + [HBM],
        out_specs=VMEM,
        out_shape=pltpu.VMEM((256, 512), F32),
        scratch_shapes=[
            pltpu.VMEM((512, 256), F32),
            pltpu.VMEM((2, 512, 512), F32),
            pltpu.SemaphoreType.DMA,
        ],
        name="tail",
        compiler_params=SMALL,
    )(me, owners, held(base), held(second), held(mine), held(other), held(inverse), in_hbm(panel))


def half_kernel(me_ref, current_ref, out_ref):
    core = me_ref[0] & 1
    for j in range(16):
        out_ref[j] = current_ref[j, 1 - core]


def half(me, current):
    return pl.pallas_call(
        half_kernel,
        in_specs=[SMEM, VMEM],
        out_specs=VMEM,
        out_shape=pltpu.VMEM((16, 8, 512), F32),
        name="half",
        compiler_params=SMALL,
    )(me, held(current))


def combine_kernel(me_ref, owners_ref, current_ref, got_ref, update_ref, out_ref):
    me = me_ref[0]
    core = me & 1
    later = (owners_ref[0] != me) & (owners_ref[1] != me)
    for j in range(16):
        own, got = current_ref[j, core], got_ref[j]
        for m in range(2):
            d = 2 * j + m
            value = jnp.where(later, jnp.where(core == m, own, got), 0.0) - update_ref[8 * d : 8 * d + 8, :]
            out_ref[0, 4 * d : 4 * d + 4, :] = value[0:4]
            out_ref[1, 4 * d : 4 * d + 4, :] = value[4:8]


def combine(me, owners, current, got, update):
    return pl.pallas_call(
        combine_kernel,
        in_specs=[SMEM, SMEM] + [VMEM] * 3,
        out_specs=VMEM,
        out_shape=jax.ShapeDtypeStruct((2, 128, 512), F32),
        name="combine",
        compiler_params=SMALL,
    )(me, owners, held(current), held(got), held(update))


def exchange(v, axis):
    return lax.all_to_all(v, axis, 0, 0, tiled=True)


def collect(v, axis):
    parts = [v]
    for k in range(1, 4):
        parts.append(lax.ppermute(v, axis, [(i, i ^ k) for i in range(4)]))
    return jnp.stack(parts)


def swap(v):
    return lax.ppermute(v, "c", [(0, 1), (1, 0)])


def shards(rhs_in, pivots, owners, panel_first, panel_second, inverse_first, inverse_second):
    row = ("z", "x", "c")
    me = lax.axis_index(row).astype(jnp.int32).reshape(1)
    place = lax.axis_index("y").astype(jnp.int32).reshape(1)
    rhs = rhs_in.reshape(2, 4, 128, 128).transpose(0, 2, 1, 3)
    piv = pivots.reshape(32, 1, 512)

    left, pieces, mine = head(place, panel_first.reshape(2, 64, 8, 512), rhs, piv, inverse_first)
    gathered = collect(mine, "z")
    pieces = exchange(pieces, row)
    gathered = collect(gathered, "x")
    blocks = gather(owners, left, piv, 2, 18)
    pieces = pick(owners, pieces)
    pieces = collect(pieces, "z")
    blocks = gather(owners, left, piv, 20, 12, blocks)
    other = swap(gathered)
    pieces = collect(pieces, "y")
    current = exchange(blocks.reshape(16, 2, 8, 512), row[:2])
    high, low, solved, second = make_operands(me, gathered, other)
    crossed = cross(me, place, pieces, high, low)
    crossed = collect(crossed, "x")
    base = make_update(me, owners, high, low, solved, panel_first)
    send = half(me, current)
    got = swap(send)
    crossed_other = swap(crossed)
    update = tail(me, owners, base, second, crossed, crossed_other, inverse_second, panel_second)
    return combine(me, owners, current, got, update)


def solution(mesh):
    fine = Mesh(mesh.devices.reshape(4, 4, 2, 4, 2), ("z", "x", "c", "y", "h"))
    row = ("z", "x", "c")
    return jax.shard_map(
        shards,
        mesh=fine,
        in_specs=(
            P(None, ("y", "h") + row, None),
            P(),
            P(),
            P(None, row, None),
            P(None, row, None),
            P(),
            P(),
        ),
        out_specs=P(None, ("y", "h"), row),
        check_vma=False,
    )
```

```python
import functools

import jax
import jax.numpy as jnp
from jax import lax
from jax.experimental import pallas as pl
from jax.experimental.pallas import tpu as pltpu
from jax.sharding import Mesh, PartitionSpec as P


F32 = jnp.float32
BF16 = jnp.bfloat16
NT = (((1,), (1,)), ((), ()))
NN = (((1,), (0,)), ((), ()))


def split(v):
    high = v.astype(BF16)
    return high, (v - high.astype(F32)).astype(BF16)


def turned(v):
    tiles = v.reshape(v.shape[0] // 8, 8, v.shape[1])
    row = lax.broadcasted_iota(jnp.int32, tiles.shape, 1)
    swapped = pltpu.roll(tiles, 4, 1)
    return jnp.where(row < 4, -swapped, swapped).reshape(v.shape)


def dot(a, b, dims=NT):
    return lax.dot_general(a, b, dims, preferred_element_type=F32)


def gather_columns(left, pivots):
    n = pivots.shape[1]
    major = pivots >> 7
    minor = pivots & 127
    pick = (lax.broadcasted_iota(jnp.int32, (128, n), 0) == major).astype(F32).astype(BF16)
    product = dot(left, jnp.concatenate([pick, pick], 0), NN).reshape(8, 16, 8, n)
    row = lax.broadcasted_iota(jnp.int32, (8, n), 0)
    found = jnp.zeros((8, 8, n), F32)
    for j in range(16):
        found = jnp.where((row + 8 * j == minor)[None], product[:, j], found)
    return found.sum(axis=1)


VMEM = pl.BlockSpec(memory_space=pltpu.VMEM)
SMEM = pl.BlockSpec(memory_space=pltpu.SMEM)
HBM = pl.BlockSpec(memory_space=pltpu.HBM)
SMALL = pltpu.CompilerParams(vmem_limit_bytes=24 << 20)


def fetches(source, target, sem, first, count):
    rows = source.shape[1] // count
    return [
        pltpu.make_async_copy(
            source.at[:, pl.ds(rows * i, rows)], target.at[:, pl.ds(rows * i, rows)], sem.at[first + i]
        )
        for i in range(count)
    ]


def held(v):
    return pltpu.with_memory_space_constraint(v, pltpu.VMEM)


def pieces_kernel(place_ref, panel_ref, out_ref, stage_ref, sem):
    column = pl.multiple_of(128 * place_ref[0], 128)
    copies = []
    stores = []
    for k in range(8):
        source = panel_ref.at[:, pl.ds(8 * k, 8), :, pl.ds(column, 128)]
        copies.append(pltpu.make_async_copy(source, stage_ref.at[k], sem.at[k]))
        stores.append(pltpu.make_async_copy(stage_ref.at[k], out_ref.at[k], sem.at[8 + k]))
    for copy in copies:
        copy.start()
    for copy, store in zip(copies, stores):
        copy.wait()
        store.start()
    for store in stores:
        store.wait()


def make_pieces(place, panel):
    return pl.pallas_call(
        pieces_kernel,
        in_specs=[SMEM, HBM],
        out_specs=HBM,
        out_shape=pltpu.HBM((8, 2, 8, 8, 128), F32),
        scratch_shapes=[pltpu.VMEM((8, 2, 8, 8, 128), F32), pltpu.SemaphoreType.DMA((16,))],
        name="pieces",
        compiler_params=SMALL,
    )(place, in_hbm(panel))


def head_kernel(rhs_hbm, pivots_ref, inverse_ref, left_ref, own_ref, rhs_ref, sem):
    copies = fetches(rhs_hbm, rhs_ref, sem, 0, 8)
    for copy in copies:
        copy.start()
    for copy in copies:
        copy.wait()
    for part in range(2):
        for c in range(4):
            r = part * 4 + c
            high, low = split(rhs_ref[part, :, c, :].T)
            left_ref[pl.ds(128 * r, 128), 0:128] = high
            left_ref[pl.ds(128 * r, 128), 128:256] = low
    left = left_ref[...]
    first = jnp.concatenate([gather_columns(left, pivots_ref[0, :, 256 * k : 256 * k + 256]) for k in range(2)], 1)
    second = jnp.concatenate([gather_columns(left, pivots_ref[1, :, 256 * k : 256 * k + 256]) for k in range(2)], 1)
    own_ref[1] = second
    high, low = split(jnp.concatenate([first, turned(first)], 1))
    w_high, w_low = split(jnp.concatenate([inverse_ref[0], inverse_ref[1]], 1))
    both = dot(jnp.concatenate([high, low], 0), w_high)
    own_ref[0] = both[0:8] + both[8:16] + dot(high, w_low)


def in_hbm(v):
    return pltpu.with_memory_space_constraint(v, pltpu.HBM)


def head(rhs, pivots, inverse):
    return pl.pallas_call(
        head_kernel,
        in_specs=[HBM, VMEM, VMEM],
        out_specs=[VMEM] * 2,
        out_shape=[pltpu.VMEM((1024, 256), BF16), pltpu.VMEM((2, 8, 512), F32)],
        scratch_shapes=[pltpu.VMEM((2, 128, 4, 128), F32), pltpu.SemaphoreType.DMA((8,))],
        name="head",
        compiler_params=SMALL,
    )(in_hbm(rhs), held(pivots), held(inverse))


def gather_kernel(start, count, owners_ref, left_ref, pivots_ref, *rest):
    out_ref, stage_ref, sem = rest[-3:]

    def send(i):
        return pltpu.make_async_copy(stage_ref.at[i], out_ref.at[owners_ref[start + i]], sem.at[i])

    def step(i, carry):
        left = left_ref[...]
        for k in range(2):
            at = slice(256 * k, 256 * k + 256)
            stage_ref[i, :, at] = gather_columns(left, pivots_ref[start + i, :, at])
        send(i).start()
        return carry

    lax.fori_loop(0, count, step, 0, unroll=6)
    for i in range(count):
        send(i).wait()


def gather(owners, left, pivots, start, count, into=None):
    operands = [owners, held(left), pivots]
    specs = [SMEM, VMEM, VMEM]
    aliases = {}
    if into is not None:
        operands.append(into)
        specs.append(HBM)
        aliases = {3: 0}
    return pl.pallas_call(
        functools.partial(gather_kernel, start, count),
        in_specs=specs,
        out_specs=HBM,
        out_shape=pltpu.HBM((32, 8, 512), F32),
        scratch_shapes=[pltpu.VMEM((count, 8, 512), F32), pltpu.SemaphoreType.DMA((count,))],
        input_output_aliases=aliases,
        name="gather_blocks",
        compiler_params=SMALL,
    )(*operands)


def pick_kernel(owners_ref, all_ref, out_ref):
    out_ref[...] = all_ref[owners_ref[1] & 7]


def pick(owners, everything):
    return pl.pallas_call(
        pick_kernel,
        in_specs=[SMEM, VMEM],
        out_specs=VMEM,
        out_shape=pltpu.VMEM((2, 8, 8, 128), F32),
        name="pick",
        compiler_params=SMALL,
    )(owners, held(everything))


def choose_kernel(me_ref, owners_ref, own_ref, one_ref, two_ref, three_ref, out_ref):
    k = (me_ref[0] ^ owners_ref[1]) >> 3
    low = jnp.where((k & 1) == 0, own_ref[...], one_ref[...])
    high = jnp.where((k & 1) == 0, two_ref[...], three_ref[...])
    out_ref[...] = jnp.where(k < 2, low, high)


def choose(me, owners, parts):
    return pl.pallas_call(
        choose_kernel,
        in_specs=[SMEM, SMEM] + [VMEM] * 4,
        out_specs=VMEM,
        out_shape=pltpu.VMEM((2, 8, 8, 128), F32),
        name="choose",
        compiler_params=SMALL,
    )(me, owners, *[held(p) for p in parts])


def triple(high, low, ref):
    n = high.shape[0]
    w_high, w_low = split(jnp.concatenate([ref[0], ref[1]], 1))
    both = dot(jnp.concatenate([high, low], 0), w_high)
    return both[:n] + (both[n:] + dot(high, w_low))


def operands_kernel(me_ref, mine_ref, other_ref, high_ref, low_ref, solved_ref, second_hbm, second_ref, sem):
    me = me_ref[0]
    even = (me & 1) == 0

    def arranged(j, n):
        k = (me >> 1) ^ j
        k = ((k & 1) << 3) | (k & 4) | (k & 2) | (k >> 3)
        mine, other = mine_ref[k, n], other_ref[k, n]
        return jnp.concatenate([jnp.where(even, mine, other), jnp.where(even, other, mine)], 0)

    for j in range(16):
        second_ref[pl.ds(16 * j, 16), :] = arranged(j, 1)
    store = pltpu.make_async_copy(second_ref, second_hbm, sem)
    store.start()
    for j in range(16):
        at = pl.ds(16 * j, 16)
        v = arranged(j, 0)
        high, low = split(jnp.concatenate([v, turned(v)], 1))
        high_ref[at, :] = high
        low_ref[at, :] = low
        solved_ref[at, :] = v
    store.wait()


def make_operands(me, mine, other):
    return pl.pallas_call(
        operands_kernel,
        in_specs=[SMEM, VMEM, VMEM],
        out_specs=[VMEM] * 3 + [HBM],
        out_shape=[pltpu.VMEM((256, 1024), BF16)] * 2 + [pltpu.VMEM((256, 512), F32), pltpu.HBM((256, 512), F32)],
        scratch_shapes=[pltpu.VMEM((256, 512), F32), pltpu.SemaphoreType.DMA],
        name="operands",
        compiler_params=SMALL,
    )(me, held(mine.reshape(16, 2, 8, 512)), held(other.reshape(16, 2, 8, 512)))


def update_kernel(me_ref, owners_ref, high_ref, low_ref, solved_ref, panel_hbm, out_ref, panel_ref, sem):
    copies = fetches(panel_hbm, panel_ref, sem, 0, 8)
    for copy in copies:
        copy.start()
    for copy in copies:
        copy.wait()
    update = triple(high_ref[...], low_ref[...], panel_ref)
    out_ref[...] = jnp.where(owners_ref[0] == me_ref[0], -solved_ref[...], update)


def make_update(me, owners, high, low, solved, panel):
    return pl.pallas_call(
        update_kernel,
        in_specs=[SMEM, SMEM, VMEM, VMEM, VMEM, HBM],
        out_specs=VMEM,
        out_shape=pltpu.VMEM((256, 512), F32),
        scratch_shapes=[pltpu.VMEM((2, 512, 512), F32), pltpu.SemaphoreType.DMA((8,))],
        name="update",
        compiler_params=SMALL,
    )(me, owners, held(high), held(low), held(solved), in_hbm(panel))


def cross_kernel(place_ref, pieces_ref, high_ref, low_ref, out_ref, panel_ref):
    for y in range(4):
        for part in range(2):
            piece = pieces_ref[place_ref[0] ^ y, part]
            panel_ref[:, pl.ds(512 * part + 128 * y, 128)] = piece.reshape(64, 128)
    q_high, q_low = split(panel_ref[...])
    both = dot(jnp.concatenate([q_high, q_low], 0), high_ref[...])
    out_ref[...] = both[0:64] + both[64:128] + dot(q_high, low_ref[...])


def cross(place, pieces, high, low):
    return pl.pallas_call(
        cross_kernel,
        in_specs=[SMEM] + [VMEM] * 3,
        out_specs=VMEM,
        out_shape=pltpu.VMEM((64, 256), F32),
        scratch_shapes=[pltpu.VMEM((64, 1024), F32)],
        name="cross",
        compiler_params=SMALL,
    )(place, held(pieces), held(high), held(low))


def tail_kernel(
    me_ref, owners_ref, base_ref, second_hbm, mine_ref, other_ref, inverse_ref, panel_hbm, out_ref,
    cross_ref, second_ref, panel_ref, sem,
):
    fetch = pltpu.make_async_copy(second_hbm, second_ref, sem.at[8])
    copies = fetches(panel_hbm, panel_ref, sem, 0, 8)
    for copy in [fetch] + copies:
        copy.start()
    me = me_ref[0]
    core = me & 1
    for x in range(4):
        k = ((me >> 1) & 3) ^ x
        cross_ref[pl.ds(pl.multiple_of(128 * x + 64 * core, 64), 64), :] = mine_ref[k]
        cross_ref[pl.ds(pl.multiple_of(128 * x + 64 - 64 * core, 64), 64), :] = other_ref[k]

    def product(value, ref):
        return triple(*split(jnp.concatenate([value, turned(value)], 1)), ref)

    crossed = cross_ref[...].T
    fetch.wait()
    solved = product(second_ref[...] - crossed, inverse_ref)
    for copy in copies:
        copy.wait()
    update = base_ref[...] + jnp.where(owners_ref[0] == me, 0.0, product(solved, panel_ref))
    out_ref[...] = jnp.where(owners_ref[1] == me, -solved, update)


def tail(me, owners, base, second, mine, other, inverse, panel):
    return pl.pallas_call(
        tail_kernel,
        in_specs=[SMEM, SMEM, VMEM, HBM] + [VMEM] * 3 + [HBM],
        out_specs=VMEM,
        out_shape=pltpu.VMEM((256, 512), F32),
        scratch_shapes=[
            pltpu.VMEM((512, 256), F32),
            pltpu.VMEM((256, 512), F32),
            pltpu.VMEM((2, 512, 512), F32),
            pltpu.SemaphoreType.DMA((9,)),
        ],
        name="tail",
        compiler_params=SMALL,
    )(me, owners, held(base), in_hbm(second), held(mine), held(other), held(inverse), in_hbm(panel))


def half_kernel(me_ref, current_ref, out_ref):
    core = me_ref[0] & 1
    for j in range(16):
        out_ref[j] = current_ref[j, 1 - core]


def half(me, current):
    return pl.pallas_call(
        half_kernel,
        in_specs=[SMEM, VMEM],
        out_specs=VMEM,
        out_shape=pltpu.VMEM((16, 8, 512), F32),
        name="half",
        compiler_params=SMALL,
    )(me, held(current))


def combine_kernel(me_ref, owners_ref, current_ref, got_ref, update_ref, out_ref, stage_ref, sem):
    me = me_ref[0]
    core = me & 1
    later = (owners_ref[0] != me) & (owners_ref[1] != me)
    stores = []
    for j in range(16):
        own, got = current_ref[j, core], got_ref[j]
        for m in range(2):
            d = 2 * j + m
            value = jnp.where(later, jnp.where(core == m, own, got), 0.0) - update_ref[8 * d : 8 * d + 8, :]
            stage_ref[0, 4 * d : 4 * d + 4, :] = value[0:4]
            stage_ref[1, 4 * d : 4 * d + 4, :] = value[4:8]
        if j % 4 == 3:
            rows = pl.ds(8 * j - 24, 32)
            stores.append(pltpu.make_async_copy(stage_ref.at[:, rows], out_ref.at[:, rows], sem.at[j // 4]))
            stores[-1].start()
    for store in stores:
        store.wait()


def combine(me, owners, current, got, update):
    return pl.pallas_call(
        combine_kernel,
        in_specs=[SMEM, SMEM] + [VMEM] * 3,
        out_specs=HBM,
        out_shape=pltpu.HBM((2, 128, 512), F32),
        scratch_shapes=[pltpu.VMEM((2, 128, 512), F32), pltpu.SemaphoreType.DMA((4,))],
        name="combine",
        compiler_params=SMALL,
    )(me, owners, held(current), held(got), held(update))


ONE, TWO = 6, 12


def exchange(v, axis):
    return lax.all_to_all(v, axis, 0, 0, tiled=True)


def parts_of(v, axis):
    parts = [v]
    for k in range(1, 4):
        parts.append(lax.ppermute(v, axis, [(i, i ^ k) for i in range(4)]))
    return parts


def double(v, axis, k):
    other = lax.ppermute(v, axis, [(i, i ^ k) for i in range(4)])
    return jnp.stack([v, other])


def collect(v, axis):
    return jnp.stack(parts_of(v, axis))


def swap(v):
    return lax.ppermute(v, "c", [(0, 1), (1, 0)])


def shards(rhs_in, pivots, owners, panel_first, panel_second, inverse_first, inverse_second):
    row = ("z", "x", "c")
    me = lax.axis_index(row).astype(jnp.int32).reshape(1)
    place = lax.axis_index("y").astype(jnp.int32).reshape(1)
    rhs = rhs_in.reshape(2, 4, 128, 128).transpose(0, 2, 1, 3)
    piv = pivots.reshape(32, 1, 512)

    pieces = make_pieces(place, panel_first.reshape(2, 64, 8, 512))
    pieces = exchange(pieces, row[1:])
    left, gathered = head(rhs, piv, inverse_first)
    gathered = double(gathered, "z", 2)
    blocks = gather(owners, left, piv, 2, ONE)
    gathered = double(gathered, "x", 2)
    piece = pick(owners, pieces)
    parts = parts_of(piece, "z")
    blocks = gather(owners, left, piv, 2 + ONE, TWO, blocks)
    gathered = double(gathered, "z", 1)
    piece = choose(me, owners, parts)
    pieces = collect(piece, "y")
    gathered = double(gathered, "x", 1)
    blocks = gather(owners, left, piv, 2 + ONE + TWO, 30 - ONE - TWO, blocks)
    other = swap(gathered)
    current = exchange(blocks.reshape(16, 2, 8, 512), row[:2])
    high, low, solved, second = make_operands(me, gathered, other)
    crossed = cross(place, pieces, high, low)
    crossed = collect(crossed, "x")
    base = make_update(me, owners, high, low, solved, panel_first)
    send = half(me, current)
    got = swap(send)
    crossed_other = swap(crossed)
    update = tail(me, owners, base, second, crossed, crossed_other, inverse_second, panel_second)
    return combine(me, owners, current, got, update)


def solution(mesh):
    fine = Mesh(mesh.devices.reshape(4, 4, 2, 4, 2), ("z", "x", "c", "y", "h"))
    row = ("z", "x", "c")
    return jax.shard_map(
        shards,
        mesh=fine,
        in_specs=(
            P(None, ("y", "h") + row, None),
            P(),
            P(),
            P(None, row, None),
            P(None, row, None),
            P(),
            P(),
        ),
        out_specs=P(None, ("y", "h"), row),
        check_vma=False,
    )
```

```python
import functools

import jax
import jax.numpy as jnp
from jax import lax
from jax.experimental import pallas as pl
from jax.experimental.pallas import tpu as pltpu
from jax.sharding import Mesh, PartitionSpec as P


F32 = jnp.float32
BF16 = jnp.bfloat16
NT = (((1,), (1,)), ((), ()))
NN = (((1,), (0,)), ((), ()))


def split(v):
    high = v.astype(BF16)
    return high, (v - high.astype(F32)).astype(BF16)


def turned(v):
    tiles = v.reshape(v.shape[0] // 8, 8, v.shape[1])
    row = lax.broadcasted_iota(jnp.int32, tiles.shape, 1)
    swapped = pltpu.roll(tiles, 4, 1)
    return jnp.where(row < 4, -swapped, swapped).reshape(v.shape)


def dot(a, b, dims=NT):
    return lax.dot_general(a, b, dims, preferred_element_type=F32)


def gather_columns(left, pivots):
    n = pivots.shape[1]
    major = pivots >> 7
    minor = pivots & 127
    pick = (lax.broadcasted_iota(jnp.int32, (128, n), 0) == major).astype(F32).astype(BF16)
    product = dot(left, jnp.concatenate([pick, pick], 0), NN).reshape(8, 16, 8, n)
    row = lax.broadcasted_iota(jnp.int32, (8, n), 0)
    found = jnp.zeros((8, 8, n), F32)
    for j in range(16):
        found = jnp.where((row + 8 * j == minor)[None], product[:, j], found)
    return found.sum(axis=1)


VMEM = pl.BlockSpec(memory_space=pltpu.VMEM)
SMEM = pl.BlockSpec(memory_space=pltpu.SMEM)
HBM = pl.BlockSpec(memory_space=pltpu.HBM)
SMALL = pltpu.CompilerParams(vmem_limit_bytes=24 << 20)


def fetches(source, target, sem, first, count):
    rows = source.shape[1] // count
    return [
        pltpu.make_async_copy(
            source.at[:, pl.ds(rows * i, rows)], target.at[:, pl.ds(rows * i, rows)], sem.at[first + i]
        )
        for i in range(count)
    ]


def held(v):
    return pltpu.with_memory_space_constraint(v, pltpu.VMEM)


def pieces_kernel(place_ref, panel_ref, out_ref, stage_ref, sem):
    column = pl.multiple_of(128 * place_ref[0], 128)
    copies = []
    stores = []
    for k in range(8):
        source = panel_ref.at[:, pl.ds(8 * k, 8), :, pl.ds(column, 128)]
        copies.append(pltpu.make_async_copy(source, stage_ref.at[k], sem.at[k]))
        stores.append(pltpu.make_async_copy(stage_ref.at[k], out_ref.at[k], sem.at[8 + k]))
    for copy in copies:
        copy.start()
    for copy, store in zip(copies, stores):
        copy.wait()
        store.start()
    for store in stores:
        store.wait()


def make_pieces(place, panel):
    return pl.pallas_call(
        pieces_kernel,
        in_specs=[SMEM, HBM],
        out_specs=HBM,
        out_shape=pltpu.HBM((8, 2, 8, 8, 128), F32),
        scratch_shapes=[pltpu.VMEM((8, 2, 8, 8, 128), F32), pltpu.SemaphoreType.DMA((16,))],
        name="pieces",
        compiler_params=SMALL,
    )(place, in_hbm(panel))


def head_kernel(rhs_hbm, pivots_ref, inverse_ref, left_ref, own_ref, rhs_ref, sem):
    copies = fetches(rhs_hbm, rhs_ref, sem, 0, 8)
    for copy in copies:
        copy.start()
    for copy in copies:
        copy.wait()
    for part in range(2):
        for c in range(4):
            r = part * 4 + c
            high, low = split(rhs_ref[part, :, c, :].T)
            left_ref[pl.ds(128 * r, 128), 0:128] = high
            left_ref[pl.ds(128 * r, 128), 128:256] = low
    left = left_ref[...]
    first = jnp.concatenate([gather_columns(left, pivots_ref[0, :, 256 * k : 256 * k + 256]) for k in range(2)], 1)
    second = jnp.concatenate([gather_columns(left, pivots_ref[1, :, 256 * k : 256 * k + 256]) for k in range(2)], 1)
    own_ref[1] = second
    high, low = split(jnp.concatenate([first, turned(first)], 1))
    w_high, w_low = split(jnp.concatenate([inverse_ref[0], inverse_ref[1]], 1))
    both = dot(jnp.concatenate([high, low], 0), w_high)
    own_ref[0] = both[0:8] + both[8:16] + dot(high, w_low)


def in_hbm(v):
    return pltpu.with_memory_space_constraint(v, pltpu.HBM)


def head(rhs, pivots, inverse):
    return pl.pallas_call(
        head_kernel,
        in_specs=[HBM, VMEM, VMEM],
        out_specs=[VMEM] * 2,
        out_shape=[pltpu.VMEM((1024, 256), BF16), pltpu.VMEM((2, 8, 512), F32)],
        scratch_shapes=[pltpu.VMEM((2, 128, 4, 128), F32), pltpu.SemaphoreType.DMA((8,))],
        name="head",
        compiler_params=SMALL,
    )(in_hbm(rhs), held(pivots), held(inverse))


def gather_kernel(start, count, owners_ref, left_ref, pivots_ref, *rest):
    out_ref, stage_ref, sem = rest[-3:]

    def send(i):
        return pltpu.make_async_copy(stage_ref.at[i], out_ref.at[owners_ref[start + i]], sem.at[i])

    def step(i, carry):
        left = left_ref[...]
        for k in range(2):
            at = slice(256 * k, 256 * k + 256)
            stage_ref[i, :, at] = gather_columns(left, pivots_ref[start + i, :, at])
        send(i).start()
        return carry

    lax.fori_loop(0, count, step, 0, unroll=min(count, 12))
    for i in range(count):
        send(i).wait()


def gather(owners, left, pivots, start, count, into=None):
    operands = [owners, held(left), pivots]
    specs = [SMEM, VMEM, VMEM]
    aliases = {}
    if into is not None:
        operands.append(into)
        specs.append(HBM)
        aliases = {3: 0}
    return pl.pallas_call(
        functools.partial(gather_kernel, start, count),
        in_specs=specs,
        out_specs=HBM,
        out_shape=pltpu.HBM((32, 8, 512), F32),
        scratch_shapes=[pltpu.VMEM((count, 8, 512), F32), pltpu.SemaphoreType.DMA((count,))],
        input_output_aliases=aliases,
        name="gather_blocks",
        compiler_params=SMALL,
    )(*operands)


def pick_kernel(owners_ref, all_ref, out_ref):
    out_ref[...] = all_ref[owners_ref[1] & 7]


def pick(owners, everything):
    return pl.pallas_call(
        pick_kernel,
        in_specs=[SMEM, VMEM],
        out_specs=VMEM,
        out_shape=pltpu.VMEM((2, 8, 8, 128), F32),
        name="pick",
        compiler_params=SMALL,
    )(owners, held(everything))


def choose_kernel(me_ref, owners_ref, own_ref, one_ref, two_ref, three_ref, out_ref):
    k = (me_ref[0] ^ owners_ref[1]) >> 3
    low = jnp.where((k & 1) == 0, own_ref[...], one_ref[...])
    high = jnp.where((k & 1) == 0, two_ref[...], three_ref[...])
    out_ref[...] = jnp.where(k < 2, low, high)


def choose(me, owners, parts):
    return pl.pallas_call(
        choose_kernel,
        in_specs=[SMEM, SMEM] + [VMEM] * 4,
        out_specs=VMEM,
        out_shape=pltpu.VMEM((2, 8, 8, 128), F32),
        name="choose",
        compiler_params=SMALL,
    )(me, owners, *[held(p) for p in parts])


def triple(high, low, ref):
    n = high.shape[0]
    w_high, w_low = split(jnp.concatenate([ref[0], ref[1]], 1))
    both = dot(jnp.concatenate([high, low], 0), w_high)
    return both[:n] + (both[n:] + dot(high, w_low))


def operands_kernel(me_ref, mine_ref, other_ref, high_ref, low_ref, solved_ref, second_hbm, second_ref, sem):
    me = me_ref[0]
    even = (me & 1) == 0

    def arranged(j, n):
        k = (me >> 1) ^ j
        k = ((k & 1) << 3) | (k & 4) | (k & 2) | (k >> 3)
        mine, other = mine_ref[k, n], other_ref[k, n]
        return jnp.concatenate([jnp.where(even, mine, other), jnp.where(even, other, mine)], 0)

    for j in range(16):
        second_ref[pl.ds(16 * j, 16), :] = arranged(j, 1)
    store = pltpu.make_async_copy(second_ref, second_hbm, sem)
    store.start()
    for j in range(16):
        at = pl.ds(16 * j, 16)
        v = arranged(j, 0)
        high, low = split(jnp.concatenate([v, turned(v)], 1))
        high_ref[at, :] = high
        low_ref[at, :] = low
        solved_ref[at, :] = v
    store.wait()


def make_operands(me, mine, other):
    return pl.pallas_call(
        operands_kernel,
        in_specs=[SMEM, VMEM, VMEM],
        out_specs=[VMEM] * 3 + [HBM],
        out_shape=[pltpu.VMEM((256, 1024), BF16)] * 2 + [pltpu.VMEM((256, 512), F32), pltpu.HBM((256, 512), F32)],
        scratch_shapes=[pltpu.VMEM((256, 512), F32), pltpu.SemaphoreType.DMA],
        name="operands",
        compiler_params=SMALL,
    )(me, held(mine.reshape(16, 2, 8, 512)), held(other.reshape(16, 2, 8, 512)))


def update_kernel(me_ref, owners_ref, high_ref, low_ref, solved_ref, panel_hbm, out_ref, panel_ref, sem):
    copies = fetches(panel_hbm, panel_ref, sem, 0, 8)
    for copy in copies:
        copy.start()
    for copy in copies:
        copy.wait()
    update = triple(high_ref[...], low_ref[...], panel_ref)
    out_ref[...] = jnp.where(owners_ref[0] == me_ref[0], -solved_ref[...], update)


def make_update(me, owners, high, low, solved, panel):
    return pl.pallas_call(
        update_kernel,
        in_specs=[SMEM, SMEM, VMEM, VMEM, VMEM, HBM],
        out_specs=VMEM,
        out_shape=pltpu.VMEM((256, 512), F32),
        scratch_shapes=[pltpu.VMEM((2, 512, 512), F32), pltpu.SemaphoreType.DMA((8,))],
        name="update",
        compiler_params=SMALL,
    )(me, owners, held(high), held(low), held(solved), in_hbm(panel))


def cross_kernel(place_ref, pieces_ref, high_ref, low_ref, out_ref, panel_ref):
    for y in range(4):
        for part in range(2):
            piece = pieces_ref[place_ref[0] ^ y, part]
            panel_ref[:, pl.ds(512 * part + 128 * y, 128)] = piece.reshape(64, 128)
    q_high, q_low = split(panel_ref[...])
    both = dot(jnp.concatenate([q_high, q_low], 0), high_ref[...])
    out_ref[...] = both[0:64] + both[64:128] + dot(q_high, low_ref[...])


def cross(place, pieces, high, low):
    return pl.pallas_call(
        cross_kernel,
        in_specs=[SMEM] + [VMEM] * 3,
        out_specs=VMEM,
        out_shape=pltpu.VMEM((64, 256), F32),
        scratch_shapes=[pltpu.VMEM((64, 1024), F32)],
        name="cross",
        compiler_params=SMALL,
    )(place, held(pieces), held(high), held(low))


def tail_kernel(
    me_ref, owners_ref, base_ref, second_hbm, mine_ref, other_ref, inverse_ref, panel_hbm, out_ref,
    cross_ref, second_ref, panel_ref, sem,
):
    fetch = pltpu.make_async_copy(second_hbm, second_ref, sem.at[8])
    copies = fetches(panel_hbm, panel_ref, sem, 0, 8)
    for copy in [fetch] + copies:
        copy.start()
    me = me_ref[0]
    core = me & 1
    for x in range(4):
        k = ((me >> 1) & 3) ^ x
        cross_ref[pl.ds(pl.multiple_of(128 * x + 64 * core, 64), 64), :] = mine_ref[k]
        cross_ref[pl.ds(pl.multiple_of(128 * x + 64 - 64 * core, 64), 64), :] = other_ref[k]

    def product(value, ref):
        return triple(*split(jnp.concatenate([value, turned(value)], 1)), ref)

    crossed = cross_ref[...].T
    fetch.wait()
    solved = product(second_ref[...] - crossed, inverse_ref)
    for copy in copies:
        copy.wait()
    update = base_ref[...] + jnp.where(owners_ref[0] == me, 0.0, product(solved, panel_ref))
    out_ref[...] = jnp.where(owners_ref[1] == me, -solved, update)


def tail(me, owners, base, second, mine, other, inverse, panel):
    return pl.pallas_call(
        tail_kernel,
        in_specs=[SMEM, SMEM, VMEM, HBM] + [VMEM] * 3 + [HBM],
        out_specs=VMEM,
        out_shape=pltpu.VMEM((256, 512), F32),
        scratch_shapes=[
            pltpu.VMEM((512, 256), F32),
            pltpu.VMEM((256, 512), F32),
            pltpu.VMEM((2, 512, 512), F32),
            pltpu.SemaphoreType.DMA((9,)),
        ],
        name="tail",
        compiler_params=SMALL,
    )(me, owners, held(base), in_hbm(second), held(mine), held(other), held(inverse), in_hbm(panel))


def combine_kernel(me_ref, owners_ref, current_ref, update_ref, out_ref, stage_ref, sem):
    me = me_ref[0]
    later = (owners_ref[0] != me) & (owners_ref[1] != me)
    stores = []
    for d in range(32):
        value = jnp.where(later, current_ref[d], 0.0) - update_ref[8 * d : 8 * d + 8, :]
        stage_ref[0, 4 * d : 4 * d + 4, :] = value[0:4]
        stage_ref[1, 4 * d : 4 * d + 4, :] = value[4:8]
        if d % 8 == 7:
            rows = pl.ds(4 * d - 28, 32)
            stores.append(pltpu.make_async_copy(stage_ref.at[:, rows], out_ref.at[:, rows], sem.at[d // 8]))
            stores[-1].start()
    for store in stores:
        store.wait()


def combine(me, owners, current, update):
    return pl.pallas_call(
        combine_kernel,
        in_specs=[SMEM, SMEM] + [VMEM] * 2,
        out_specs=HBM,
        out_shape=pltpu.HBM((2, 128, 512), F32),
        scratch_shapes=[pltpu.VMEM((2, 128, 512), F32), pltpu.SemaphoreType.DMA((4,))],
        name="combine",
        compiler_params=SMALL,
    )(me, owners, held(current), held(update))


ONE, TWO = 6, 12


def exchange(v, axis):
    return lax.all_to_all(v, axis, 0, 0, tiled=True)


def parts_of(v, axis):
    parts = [v]
    for k in range(1, 4):
        parts.append(lax.ppermute(v, axis, [(i, i ^ k) for i in range(4)]))
    return parts


def double(v, axis, k):
    other = lax.ppermute(v, axis, [(i, i ^ k) for i in range(4)])
    return jnp.stack([v, other])


def collect(v, axis):
    return jnp.stack(parts_of(v, axis))


def swap(v):
    return lax.ppermute(v, "c", [(0, 1), (1, 0)])


def shards(rhs_in, pivots, owners, panel_first, panel_second, inverse_first, inverse_second):
    row = ("z", "x", "c")
    me = lax.axis_index(row).astype(jnp.int32).reshape(1)
    place = lax.axis_index("y").astype(jnp.int32).reshape(1)
    rhs = rhs_in.reshape(2, 4, 128, 128).transpose(0, 2, 1, 3)
    piv = pivots.reshape(32, 1, 512)

    pieces = make_pieces(place, panel_first.reshape(2, 64, 8, 512))
    pieces = exchange(pieces, row[1:])
    left, gathered = head(rhs, piv, inverse_first)
    gathered = double(gathered, "z", 2)
    blocks = gather(owners, left, piv, 2, ONE)
    gathered = double(gathered, "x", 2)
    piece = pick(owners, pieces)
    parts = parts_of(piece, "z")
    blocks = gather(owners, left, piv, 2 + ONE, TWO, blocks)
    gathered = double(gathered, "z", 1)
    piece = choose(me, owners, parts)
    pieces = collect(piece, "y")
    gathered = double(gathered, "x", 1)
    blocks = gather(owners, left, piv, 2 + ONE + TWO, 30 - ONE - TWO, blocks)
    other = swap(gathered)
    current = exchange(blocks, row)
    high, low, solved, second = make_operands(me, gathered, other)
    crossed = cross(place, pieces, high, low)
    crossed = collect(crossed, "x")
    base = make_update(me, owners, high, low, solved, panel_first)
    crossed_other = swap(crossed)
    update = tail(me, owners, base, second, crossed, crossed_other, inverse_second, panel_second)
    return combine(me, owners, current, update)


def solution(mesh):
    fine = Mesh(mesh.devices.reshape(4, 4, 2, 4, 2), ("z", "x", "c", "y", "h"))
    row = ("z", "x", "c")
    return jax.shard_map(
        shards,
        mesh=fine,
        in_specs=(
            P(None, ("y", "h") + row, None),
            P(),
            P(),
            P(None, row, None),
            P(None, row, None),
            P(),
            P(),
        ),
        out_specs=P(None, ("y", "h"), row),
        check_vma=False,
    )
```
